32 devices in a mesh: row: 2 (over y), col: 16 (over z, x, core).
Axes of the slice: x: 2, y: 2, z: 4, core: 2. Of those that a mesh axis runs over, the one named last changes fastest.
Arguments:
- object_field: float32 [2, 512, 4096], P(None, 'row', 'col'), may hold values from -5 to 5
- probe: float32 [2, 2, 256, 256], replicated, may hold values from -5 to 5
- amplitudes: float32 [2, 16, 1, 256, 256], P('row', 'col'), may hold values from 0.5 to 3
- offsets: int32 [2, 16, 1, 2], P('row', 'col'), may hold values from 0 to 128
Outputs:
- new_object: float32 [2, 512, 4096], P(None, 'row', 'col')
- new_probe: float32 [2, 2, 256, 256], replicated
The draws below stay inside these ranges and needn't reach their ends.
All inputs are finite; a program needn't handle non-finite values.
Results may differ from the reference program's by a relative error of at most 0.0003.
Values sent between devices are 32-bit elements; how exact they have to be, the bound alone decides.
A program may use at most 64 MiB of HBM per device.

```python
import jax
import jax.numpy as jnp
from jax import lax

TILE = 256
H = 64
F = 256
M = 2
POS = 1
ITERS = 2
NR = 512
NC = 4096
N_ROW = 2
N_COL = 16


def plant(values, own_key, low, high):
    index_at = [jax.random.randint(jax.random.fold_in(own_key, axis), (), 0, length) for axis, length in enumerate(values.shape)]
    main_axis = values.shape.index(max(values.shape))
    neighbour = index_at[:main_axis] + [(index_at[main_axis] + 1) % values.shape[main_axis]] + index_at[main_axis + 1:]
    return values.at[tuple(index_at)].set(low).at[tuple(neighbour)].set(high)


def levels(own_key, extent, cuts, smallest, largest):
    loudness = 1.0
    for position, shards_of in cuts:
        steps = jax.random.uniform(jax.random.fold_in(jax.random.fold_in(own_key, 6), position), (shards_of,), jnp.float32, smallest / len(cuts), largest / len(cuts))
        loudness = loudness * jnp.repeat(jnp.exp(steps), extent[position] // shards_of).reshape((-1,) + (1,) * (len(extent) - 1 - position))
    return loudness


def bell_draw(own_key, shape, deviation, reach, cuts=(), kind=jnp.bfloat16):
    values = deviation * jax.random.normal(own_key, shape, jnp.float32)
    if cuts:
        values = values * levels(own_key, shape, cuts, -0.22, 0.18)
    return jnp.clip(values, -reach, reach).astype(kind)


def setup_inputs(seed: int = 0) -> dict:
    splits = jax.random.split(jax.random.key(seed), 5)
    object_field = bell_draw(splits[0], (2, NR, NC), 0.7, 5.0, ((1, 2), (2, 16)), jnp.float32)
    probe = bell_draw(splits[1], (2, M, F, F), 0.7, 5.0, (), jnp.float32)
    amplitudes = jnp.clip(0.5 + 2.5 * jax.random.uniform(splits[2], (N_ROW, N_COL, POS, F, F), jnp.float32) ** levels(splits[2], (N_ROW, N_COL, POS, F, F), ((0, 2), (1, 16)), -0.2, 0.2), 0.5, 3.0)
    offsets = plant(jax.random.randint(splits[3], (N_ROW, N_COL, POS, 2), 0, TILE + 2 * H - F + 1), jax.random.fold_in(splits[3], 1), 0, TILE + 2 * H - F).astype(jnp.int32)
    return dict(object_field=object_field, probe=probe, amplitudes=amplitudes, offsets=offsets)


object_step = 0.25
probe_step = 4.0

def transform(real_part, imag_part, inverse):
    field = lax.complex(real_part, imag_part)
    if inverse:
        result = jnp.fft.ifft2(field, norm='ortho')
    else:
        result = jnp.fft.fft2(field, norm='ortho')
    return (jnp.real(result), jnp.imag(result))

def frame_terms(patch, probe, measured):
    probe_re, probe_im = (probe[0], probe[1])
    wave_re = probe_re * patch[0] - probe_im * patch[1]
    wave_im = probe_re * patch[1] + probe_im * patch[0]
    far_re, far_im = transform(wave_re, wave_im, False)
    intensity = lax.optimization_barrier(jnp.sum(far_re * far_re + far_im * far_im, axis=0))
    factor = 1.0 - measured / jnp.sqrt(intensity + 1.0)
    back_re, back_im = transform(far_re * factor, far_im * factor, True)
    object_re = lax.optimization_barrier(jnp.sum(probe_re * back_re + probe_im * back_im, axis=0))
    object_im = lax.optimization_barrier(jnp.sum(probe_re * back_im - probe_im * back_re, axis=0))
    probe_term_re = patch[0] * back_re + patch[1] * back_im
    probe_term_im = patch[0] * back_im - patch[1] * back_re
    return (jnp.stack([object_re, object_im]), jnp.stack([probe_term_re, probe_term_im]))

def reference(object_field, probe, amplitudes, offsets):
    frames = POS * N_ROW * N_COL
    row_base = (jnp.arange(N_ROW, dtype=jnp.int32) * TILE)[:, None, None]
    col_base = (jnp.arange(N_COL, dtype=jnp.int32) * TILE)[None, :, None]
    rows_at = (row_base + offsets[:, :, :, 0]).reshape(-1).astype(jnp.int32)
    cols_at = (col_base + offsets[:, :, :, 1]).reshape(-1).astype(jnp.int32)
    measured_all = amplitudes.reshape(-1, F, F)
    zero = jnp.zeros((), jnp.int32)

    def one_iteration(current, probes):
        padded = jnp.pad(current, ((0, 0), (H, H), (H, H)))

        def visit(carry, item):
            grad_pad, probe_grad = carry
            row_at, col_at, measured = item
            start = (zero, row_at.astype(jnp.int32), col_at.astype(jnp.int32))
            patch = lax.dynamic_slice(padded, start, (2, F, F))
            term_object, term_probe = frame_terms(patch, probes, measured)
            window = lax.dynamic_slice(grad_pad, start, (2, F, F))
            grad_pad = lax.dynamic_update_slice(grad_pad, window + term_object, start)
            return ((grad_pad, probe_grad + term_probe), None)
        (grad_pad, probe_grad), _ = lax.scan(visit, (jnp.zeros_like(padded), jnp.zeros_like(probes)), (rows_at, cols_at, measured_all))
        object_grad = grad_pad[:, H:H + NR, H:H + NC]
        return (current - object_step * object_grad, probes - probe_step / frames * probe_grad)
    current, probes = (object_field, probe)
    for iteration in range(ITERS):
        current, probes = one_iteration(current, probes)
    return (current, probes)
```

```python
import functools
import math

import jax
import jax.numpy as jnp
import numpy as np
from jax import lax
from jax.experimental import pallas as pl
from jax.experimental.pallas import tpu as pltpu
from jax.sharding import PartitionSpec as P

H = 64
LANES = 128
ITERS = 2
object_step = 0.25
probe_step = 4.0
MESH = pl.DeviceIdType.MESH
bf16 = jnp.bfloat16


def dft_tables(length):
    counter = np.arange(length)
    angle = -2.0 * math.pi / length * (counter[:, None] * counter[None, :] % length)
    scale = 1.0 / math.sqrt(length)
    parts = []
    for table in (np.cos(angle) * scale, np.sin(angle) * scale):
        table = table.astype(np.float32)
        high = table.astype(bf16)
        low = (table - high.astype(np.float32)).astype(bf16)
        parts += [high, low]
    return np.stack(parts)


def split(value):
    high = value.astype(bf16)
    return high, (value - high.astype(jnp.float32)).astype(bf16)


def product(left, right):
    out = jnp.dot(left[0][...], right[0][...], preferred_element_type=jnp.float32)
    out += jnp.dot(left[0][...], right[1][...], preferred_element_type=jnp.float32)
    return out + jnp.dot(left[1][...], right[0][...], preferred_element_type=jnp.float32)


def pick(one_hot, value):
    if isinstance(value, tuple):
        return sum(jnp.dot(one_hot[...], v, preferred_element_type=jnp.float32) for v in value)
    return sum(jnp.dot(v, value[...], preferred_element_type=jnp.float32) for v in one_hot)


def kernel(
    rows, cols, obj_ref, probe_ref, amp_ref, tables_ref, off_ref,
    new_obj_ref, new_probe_ref,
    a_hi, a_lo, b_hi, b_lo, x_hi, x_lo,
    row_pick, col_pick, row_place, col_place, ext, side, pack, grad, gpack, grows, gside, gcorner, current,
    terms, r1, a1, r2, a2, r3, weights,
    halo_send, halo_recv, grad_send, grad_recv, sum_send, sum_recv,
):
    frame = amp_ref.shape[-1]
    tile = obj_ref.shape[1]
    modes = probe_ref.shape[1]
    span = tile + 2 * H
    row, col = lax.axis_index("row"), lax.axis_index("col")
    coeff = probe_step / (rows * cols)
    core = lax.rem(col, 2)
    plane = row * 2 + lax.rem(col // 2, 2)
    line = col // 4
    planes, lines = rows * 2, cols // 4

    around = [(dr, dc) for dr in (-1, 0, 1) for dc in (-1, 0, 1) if (dr, dc) != (0, 0)]

    def inside(dr, dc):
        r, c = row + dr, col + dc
        ok = jnp.bool_(True)
        if dr:
            ok = (r >= 0) & (r < rows)
        if dc:
            ok = ok & (c >= 0) & (c < cols)
        return ok

    def plane_peer(d):
        other = lax.rem(plane + d, planes)
        return (other // 2, line * 4 + lax.rem(other, 2) * 2 + core), other

    def line_peer(d):
        other = lax.rem(line + d, lines)
        return (row, other * 4 + lax.rem(col, 4)), other

    partner = (row, col + 1 - 2 * core)

    ext[...] = jnp.zeros_like(ext)
    side[...] = jnp.zeros_like(side)
    grows[...] = jnp.zeros_like(grows)
    gside[...] = jnp.zeros_like(gside)
    gcorner[...] = jnp.zeros_like(gcorner)

    barrier = pltpu.get_barrier_semaphore()
    for dr, dc in around:
        @pl.when(inside(dr, dc))
        def _(dr=dr, dc=dc):
            pl.semaphore_signal(barrier, inc=1, device_id=(row + dr, col + dc), device_id_type=MESH)
    pl.semaphore_signal(barrier, inc=1, device_id=partner, device_id_type=MESH)
    for d in range(1, planes):
        pl.semaphore_signal(barrier, inc=1, device_id=plane_peer(d)[0], device_id_type=MESH)
    for d in range(1, lines):
        pl.semaphore_signal(barrier, inc=1, device_id=line_peer(d)[0], device_id_type=MESH)

    lane = lax.broadcasted_iota(jnp.int32, (1, LANES), 1)
    lower, upper = lane < H, lane >= H

    def paired(mask, real, imag):
        return jnp.where(mask, real, pltpu.roll(imag, H, 1))

    def pack_tile(k, src):
        pack[k, 0] = paired(lower, src[0, :, :LANES], src[1, :, :LANES])
        pack[k, 1] = paired(upper, src[0, :, tile - LANES:], src[1, :, tile - LANES:])

    def halo_copy(k, src, dr, dc):
        n = around.index((dr, dc))
        if dc == 0:
            source = src.at[:, pl.ds(0 if dr < 0 else tile - H, H), :]
            target = ext.at[k, :, pl.ds(tile + H if dr < 0 else 0, H), pl.ds(LANES, tile)]
        else:
            which = 0 if dc < 0 else 1
            at, size = {-1: (0, H), 0: (0, tile), 1: (tile - H, H)}[dr]
            source = pack.at[k, which, pl.ds(at, size)]
            target = side.at[k, 1 - which, pl.ds({-1: tile + H, 0: H, 1: 0}[dr], size)]
        return pltpu.make_async_remote_copy(
            src_ref=source, dst_ref=target, send_sem=halo_send.at[k, n], recv_sem=halo_recv.at[k, n],
            device_id=(row + dr, col + dc), device_id_type=MESH)

    def grad_copy(k, dr, dc):
        n = around.index((dr, dc))
        if dc == 0:
            source = grad.at[k, :, pl.ds(0 if dr < 0 else tile + H, H), pl.ds(LANES, tile)]
            target = grows.at[k, 0 if dr > 0 else 1]
        else:
            which = 0 if dc < 0 else 1
            at, size = {-1: (0, H), 0: (H, tile), 1: (tile + H, H)}[dr]
            source = gpack.at[k, which, pl.ds(at, size)]
            if dr == 0:
                target = gside.at[k, 1 - which]
            else:
                target = gcorner.at[k, 1 - which, 0 if dr > 0 else 1]
        return pltpu.make_async_remote_copy(
            src_ref=source, dst_ref=target, send_sem=grad_send.at[k, n], recv_sem=grad_recv.at[k, n],
            device_id=(row + dr, col + dc), device_id_type=MESH)

    def start_all(make):
        for dr, dc in around:
            @pl.when(inside(dr, dc))
            def _(dr=dr, dc=dc):
                make(dr, dc).start()

    def wait_all(make, send):
        for dr, dc in around:
            if send:
                @pl.when(inside(dr, dc))
                def _(dr=dr, dc=dc):
                    make(dr, dc).wait_send()
            else:
                @pl.when(inside(-dr, -dc))
                def _(dr=dr, dc=dc):
                    make(dr, dc).wait_recv()

    pack_tile(0, obj_ref)
    tall = 1 + (row > 0).astype(jnp.int32) + (row < rows - 1).astype(jnp.int32)
    broad = 1 + (col > 0).astype(jnp.int32) + (col < cols - 1).astype(jnp.int32)
    pl.semaphore_wait(barrier, tall * broad - 1 + planes + lines - 1)
    start_all(lambda dr, dc: halo_copy(0, obj_ref, dr, dc))

    for n, (a, b) in enumerate(((a_hi, b_hi), (a_lo, b_lo))):
        real, imag = tables_ref[n], tables_ref[2 + n]
        lo, hi = pl.ds(0, frame), pl.ds(frame, frame)
        for ref, sign in ((a, 1), (b, -1)):
            ref[lo, lo] = real
            ref[hi, hi] = real
            ref[lo, hi] = -imag if sign > 0 else imag
            ref[hi, lo] = imag if sign > 0 else -imag
    half = frame // LANES
    for c in range(2):
        ext[0, c, H:H + tile, LANES:LANES + tile] = obj_ref[c]
        for m in range(modes):
            for h in range(half):
                weights[0, pl.ds(((c * modes + m) * half + h) * frame, frame)] = (
                    probe_ref[c, m, :, h * LANES:(h + 1) * LANES])

    def probe_part(k, c, m):
        base = (c * modes + m) * half
        return jnp.concatenate(
            [weights[k, pl.ds((base + h) * frame, frame)] for h in range(half)], axis=1)

    oy, ox = off_ref[0, 0, 0, 0], off_ref[0, 0, 0, 1] + (LANES - H)
    for ref, outer, shift in (
        (row_pick, 0, oy), (row_place, 1, oy), (col_pick, 1, ox), (col_place, 0, ox)
    ):
        inner_at = lax.broadcasted_iota(jnp.int32, ref.shape, outer)
        outer_at = lax.broadcasted_iota(jnp.int32, ref.shape, 1 - outer)
        ref[...] = jnp.where(outer_at == inner_at + shift, 1.0, 0.0).astype(bf16)

    for k in range(ITERS):
        source = obj_ref if k == 0 else current
        wait_all(lambda dr, dc: halo_copy(k, source, dr, dc), False)
        for s, at in ((0, 0), (1, LANES + tile)):
            block = side[k, s]
            other = pltpu.roll(block, H, 1)
            first, second = (block, other)
            ext[k, 0, :, at:at + LANES] = first
            ext[k, 1, :, at:at + LANES] = second
        patch = [
            pick(split(pick(row_pick, split(ext[k, c]))), col_pick)
            for c in range(2)
        ]

        def cut(m):
            return pl.ds(m * frame, frame)

        for m in range(modes):
            p_re, p_im = probe_part(k, 0, m), probe_part(k, 1, m)
            for c, wave in enumerate((p_re * patch[0] - p_im * patch[1], p_re * patch[1] + p_im * patch[0])):
                x_hi[cut(c), cut(m)], x_lo[cut(c), cut(m)] = split(wave)
        out = product((a_hi, a_lo), (x_hi, x_lo))
        for m in range(modes):
            for c in range(2):
                part = out[c * frame:(c + 1) * frame, m * frame:(m + 1) * frame]
                x_hi[cut(m), cut(c)], x_lo[cut(m), cut(c)] = split(part)
        far = product((x_hi, x_lo), (b_hi, b_lo))
        far = [[far[m * frame:(m + 1) * frame, c * frame:(c + 1) * frame] for c in range(2)] for m in range(modes)]
        intensity = sum(re * re + im * im for re, im in far)
        factor = 1.0 - amp_ref[0, 0, 0] / jnp.sqrt(intensity + 1.0)
        for m in range(modes):
            for c in range(2):
                x_hi[cut(m), cut(c)], x_lo[cut(m), cut(c)] = split(far[m][c] * factor)
        out = product((x_hi, x_lo), (a_hi, a_lo))
        for m in range(modes):
            for c in range(2):
                part = out[m * frame:(m + 1) * frame, c * frame:(c + 1) * frame]
                x_hi[cut(c), cut(m)], x_lo[cut(c), cut(m)] = split(part)
        back = product((b_hi, b_lo), (x_hi, x_lo))
        back = [[back[c * frame:(c + 1) * frame, m * frame:(m + 1) * frame] for c in range(2)] for m in range(modes)]

        for m in range(modes):
            re, im = back[m]
            for c, term in enumerate((patch[0] * re + patch[1] * im, patch[0] * im - patch[1] * re)):
                for h in range(half):
                    terms[k, pl.ds(((c * modes + m) * half + h) * frame, frame)] = term[:, h * LANES:(h + 1) * LANES]
        total = terms.shape[1]
        n1 = total // 2
        n2 = n1 // planes
        n3 = n2 // lines

        def remote(src, dst, slot, device):
            return pltpu.make_async_remote_copy(
                src_ref=src, dst_ref=dst, send_sem=sum_send.at[k, slot], recv_sem=sum_recv.at[k, slot],
                device_id=device, device_id_type=MESH)

        swap = remote(terms.at[k, pl.ds(pl.multiple_of((1 - core) * n1, 8), n1)], r1.at[k], 0, partner)
        swap.start()

        for c in range(2):
            acc = None
            for m in range(modes):
                p_re, p_im = probe_part(k, 0, m), probe_part(k, 1, m)
                re, im = back[m]
                term = p_re * re + p_im * im if c == 0 else p_re * im - p_im * re
                acc = term if acc is None else acc + term
            grad[k, c] = pick(split(pick(row_place, split(acc))), col_place)
        gpack[k, 0] = paired(upper, grad[k, 0, :, :LANES], grad[k, 1, :, :LANES])
        gpack[k, 1] = paired(lower, grad[k, 0, :, LANES + tile:], grad[k, 1, :, LANES + tile:])
        start_all(lambda dr, dc: grad_copy(k, dr, dc))

        swap.wait_recv()
        a1[k] = terms[k, pl.ds(pl.multiple_of(core * n1, 8), n1)] + r1[k]
        slot = 1
        scatter2 = []
        for d in range(1, planes):
            device, other = plane_peer(d)
            copy = remote(a1.at[k, pl.ds(pl.multiple_of(other * n2, 8), n2)], r2.at[k, d - 1], slot, device)
            copy.start()
            scatter2.append(copy)
            slot += 1

        wait_all(lambda dr, dc: grad_copy(k, dr, dc), False)
        target = current if k + 1 < ITERS else new_obj_ref
        for s in range(2):
            mask, at = ((lower, 0), (upper, tile - LANES))[s]
            block = gside[k, s]
            block = jnp.concatenate(
                [block[:H] + gcorner[k, s, 0], block[H:tile - H], block[tile - H:] + gcorner[k, s, 1]], axis=0)
            where = pl.ds(LANES + at, LANES)
            grad[k, 0, H:H + tile, where] += jnp.where(mask, block, 0.0)
            grad[k, 1, H:H + tile, where] += jnp.where(mask, pltpu.roll(block, H, 1), 0.0)
        grad[k, :, H:2 * H, LANES:LANES + tile] += grows[k, 0]
        grad[k, :, tile:tile + H, LANES:LANES + tile] += grows[k, 1]
        for c in range(2):
            target[c] = source[c] - object_step * grad[k, c, H:H + tile, LANES:LANES + tile]
        if k + 1 < ITERS:
            pack_tile(k + 1, current)
            start_all(lambda dr, dc: halo_copy(k + 1, current, dr, dc))
            for c in range(2):
                ext[k + 1, c, H:H + tile, LANES:LANES + tile] = current[c]

        for copy in scatter2:
            copy.wait_recv()
        value = a1[k, pl.ds(pl.multiple_of(plane * n2, 8), n2)]
        for d in range(1, planes):
            value = value + r2[k, d - 1]
        a2[k] = value
        scatter3 = []
        for d in range(1, lines):
            device, other = line_peer(d)
            copy = remote(a2.at[k, pl.ds(pl.multiple_of(other * n3, 8), n3)], r3.at[k, d - 1], slot, device)
            copy.start()
            scatter3.append(copy)
            slot += 1
        for copy in scatter3:
            copy.wait_recv()
        value = a2[k, pl.ds(pl.multiple_of(line * n3, 8), n3)]
        for d in range(1, lines):
            value = value + r3[k, d - 1]
        at1 = core * n1
        at2 = at1 + plane * n2
        at3 = at2 + line * n3
        mine = pl.ds(pl.multiple_of(at3, 8), n3)
        weights[k + 1, mine] = weights[k, mine] - coeff * value

        gathers = []
        for peers, make, at, size in (
            (lines, line_peer, at3, n3), (planes, plane_peer, at2, n2), (2, lambda d: (partner, None), at1, n1)
        ):
            block = weights.at[k + 1, pl.ds(pl.multiple_of(at, 8), size)]
            stage = []
            for d in range(1, peers):
                copy = remote(block, block, slot, make(d)[0])
                copy.start()
                stage.append(copy)
                slot += 1
            for copy in stage:
                copy.wait_recv()
            gathers += stage
        for copy in [swap] + scatter2 + scatter3 + gathers:
            copy.wait_send()
        wait_all(lambda dr, dc: halo_copy(k, source, dr, dc), True)
        wait_all(lambda dr, dc: grad_copy(k, dr, dc), True)

    for c in range(2):
        for m in range(modes):
            new_probe_ref[c, m] = probe_part(ITERS, c, m)


def local(rows, cols, object_field, probe, amplitudes, offsets):
    frame = amplitudes.shape[-1]
    tile = object_field.shape[1]
    modes = probe.shape[1]
    span, width = tile + 2 * H, tile + 2 * LANES
    tables = jnp.asarray(dft_tables(frame))
    total = 2 * modes * frame * (frame // LANES)
    planes, lines = rows * 2, cols // 4
    n1 = total // 2
    n2 = n1 // planes
    n3 = n2 // lines
    copies = 2 + 2 * (planes - 1) + 2 * (lines - 1)
    f32 = jnp.float32
    wide = 2 * frame
    vmem = pl.BlockSpec(memory_space=pltpu.VMEM)
    dma = pltpu.SemaphoreType.DMA
    return pl.pallas_call(
        functools.partial(kernel, rows, cols),
        out_shape=(
            jax.ShapeDtypeStruct(object_field.shape, f32),
            jax.ShapeDtypeStruct(probe.shape, f32),
        ),
        in_specs=[vmem] * 4 + [pl.BlockSpec(memory_space=pltpu.SMEM)],
        out_specs=(vmem, vmem),
        scratch_shapes=[
            *[pltpu.VMEM((wide, wide), bf16)] * 4,
            *[pltpu.VMEM((wide, modes * frame), bf16)] * 2,
            pltpu.VMEM((frame, span), bf16),
            pltpu.VMEM((width, frame), bf16),
            pltpu.VMEM((span, frame), bf16),
            pltpu.VMEM((frame, width), bf16),
            pltpu.VMEM((ITERS, 2, span, width), f32),
            pltpu.VMEM((ITERS, 2, span, LANES), f32),
            pltpu.VMEM((ITERS, 2, tile, LANES), f32),
            pltpu.VMEM((ITERS, 2, span, width), f32),
            pltpu.VMEM((ITERS, 2, span, LANES), f32),
            pltpu.VMEM((ITERS, 2, 2, H, tile), f32),
            pltpu.VMEM((ITERS, 2, tile, LANES), f32),
            pltpu.VMEM((ITERS, 2, 2, H, LANES), f32),
            pltpu.VMEM((2, tile, tile), f32),
            pltpu.VMEM((ITERS, total, LANES), f32),
            pltpu.VMEM((ITERS, n1, LANES), f32),
            pltpu.VMEM((ITERS, n1, LANES), f32),
            pltpu.VMEM((ITERS, planes - 1, n2, LANES), f32),
            pltpu.VMEM((ITERS, n2, LANES), f32),
            pltpu.VMEM((ITERS, lines - 1, n3, LANES), f32),
            pltpu.VMEM((ITERS + 1, total, LANES), f32),
            dma((ITERS, 8)), dma((ITERS, 8)), dma((ITERS, 8)), dma((ITERS, 8)),
            dma((ITERS, copies)), dma((ITERS, copies)),
        ],
        compiler_params=pltpu.CompilerParams(
            collective_id=0, has_side_effects=True, vmem_limit_bytes=60 * 1024 * 1024
        ),
    )(object_field, probe, amplitudes, tables, offsets)


def solution(mesh):
    rows, cols = mesh.shape["row"], mesh.shape["col"]

    def body(*args):
        return local(rows, cols, *args)

    return jax.shard_map(
        body,
        mesh=mesh,
        in_specs=(
            P(None, "row", "col"),
            P(),
            P("row", "col", None, None, None),
            P("row", "col", None, None),
        ),
        out_specs=(P(None, "row", "col"), P()),
        check_vma=False,
    )
```

```python
import functools
import math

import jax
import jax.numpy as jnp
import numpy as np
from jax import lax
from jax.experimental import pallas as pl
from jax.experimental.pallas import tpu as pltpu
from jax.sharding import PartitionSpec as P

H = 64
LANES = 128
ITERS = 2
object_step = 0.25
probe_step = 4.0
MESH = pl.DeviceIdType.MESH
bf16 = jnp.bfloat16


def dft_tables(length):
    counter = np.arange(length)
    angle = -2.0 * math.pi / length * (counter[:, None] * counter[None, :] % length)
    scale = 1.0 / math.sqrt(length)
    parts = []
    for table in (np.cos(angle) * scale, np.sin(angle) * scale):
        table = table.astype(np.float32)
        high = table.astype(bf16)
        low = (table - high.astype(np.float32)).astype(bf16)
        parts += [high, low]
    return np.stack(parts)


def split(value):
    high = value.astype(bf16)
    return high, (value - high.astype(jnp.float32)).astype(bf16)


def product(left, right):
    out = jnp.dot(left[0][...], right[0][...], preferred_element_type=jnp.float32)
    out += jnp.dot(left[0][...], right[1][...], preferred_element_type=jnp.float32)
    return out + jnp.dot(left[1][...], right[0][...], preferred_element_type=jnp.float32)


def pick(one_hot, value):
    if isinstance(value, tuple):
        return sum(jnp.dot(one_hot[...], v, preferred_element_type=jnp.float32) for v in value)
    return sum(jnp.dot(v, value[...], preferred_element_type=jnp.float32) for v in one_hot)


def kernel(
    rows, cols, obj_ref, probe_ref, amp_ref, tables_ref, off_ref,
    new_obj_ref, new_probe_ref,
    a_hi, a_lo, b_hi, b_lo, x_hi, x_lo,
    row_pick, col_pick, row_place, col_place, ext, side, pack, grad, gpack, grows, gside, gcorner, current,
    terms, r1, a1, r2, a2, r3, weights,
    halo_send, halo_recv, grad_send, grad_recv, sum_send, sum_recv,
):
    frame = amp_ref.shape[-1]
    tile = obj_ref.shape[1]
    modes = probe_ref.shape[1]
    span = tile + 2 * H
    row, col = lax.axis_index("row"), lax.axis_index("col")
    coeff = probe_step / (rows * cols)
    core = lax.rem(col, 2)
    plane = row * 2 + lax.rem(col // 2, 2)
    line = col // 4
    planes, lines = rows * 2, cols // 4

    around = [(dr, dc) for dr in (-1, 0, 1) for dc in (-1, 0, 1) if (dr, dc) != (0, 0)]

    def inside(dr, dc):
        r, c = row + dr, col + dc
        ok = jnp.bool_(True)
        if dr:
            ok = (r >= 0) & (r < rows)
        if dc:
            ok = ok & (c >= 0) & (c < cols)
        return ok

    def flip(index, d):
        bit = 1
        while bit <= d:
            if d & bit:
                index = index + bit * (1 - 2 * lax.rem(index // bit, 2))
            bit *= 2
        return index

    def plane_peer(d):
        other = flip(plane, d)
        return (other // 2, line * 4 + lax.rem(other, 2) * 2 + core), other

    def line_peer(d):
        other = flip(line, d)
        return (row, other * 4 + lax.rem(col, 4)), other

    partner = (row, col + 1 - 2 * core)

    ext[...] = jnp.zeros_like(ext)
    side[...] = jnp.zeros_like(side)
    grows[...] = jnp.zeros_like(grows)
    gside[...] = jnp.zeros_like(gside)
    gcorner[...] = jnp.zeros_like(gcorner)

    barrier = pltpu.get_barrier_semaphore()
    for dr, dc in around:
        @pl.when(inside(dr, dc))
        def _(dr=dr, dc=dc):
            pl.semaphore_signal(barrier, inc=1, device_id=(row + dr, col + dc), device_id_type=MESH)
    pl.semaphore_signal(barrier, inc=1, device_id=partner, device_id_type=MESH)
    for d in range(1, planes):
        pl.semaphore_signal(barrier, inc=1, device_id=plane_peer(d)[0], device_id_type=MESH)
    for d in range(1, lines):
        pl.semaphore_signal(barrier, inc=1, device_id=line_peer(d)[0], device_id_type=MESH)

    lane = lax.broadcasted_iota(jnp.int32, (1, LANES), 1)
    lower, upper = lane < H, lane >= H

    def paired(mask, real, imag):
        return jnp.where(mask, real, pltpu.roll(imag, H, 1))

    def pack_tile(k, src):
        pack[k, 0] = paired(lower, src[0, :, :LANES], src[1, :, :LANES])
        pack[k, 1] = paired(upper, src[0, :, tile - LANES:], src[1, :, tile - LANES:])

    def halo_copy(k, src, dr, dc):
        n = around.index((dr, dc))
        if dc == 0:
            source = src.at[:, pl.ds(0 if dr < 0 else tile - H, H), :]
            target = ext.at[k, :, pl.ds(tile + H if dr < 0 else 0, H), pl.ds(LANES, tile)]
        else:
            which = 0 if dc < 0 else 1
            at, size = {-1: (0, H), 0: (0, tile), 1: (tile - H, H)}[dr]
            source = pack.at[k, which, pl.ds(at, size)]
            target = side.at[k, 1 - which, pl.ds({-1: tile + H, 0: H, 1: 0}[dr], size)]
        return pltpu.make_async_remote_copy(
            src_ref=source, dst_ref=target, send_sem=halo_send.at[k, n], recv_sem=halo_recv.at[k, n],
            device_id=(row + dr, col + dc), device_id_type=MESH)

    def grad_copy(k, dr, dc):
        n = around.index((dr, dc))
        if dc == 0:
            source = grad.at[k, :, pl.ds(0 if dr < 0 else tile + H, H), pl.ds(LANES, tile)]
            target = grows.at[k, 0 if dr > 0 else 1]
        else:
            which = 0 if dc < 0 else 1
            at, size = {-1: (0, H), 0: (H, tile), 1: (tile + H, H)}[dr]
            source = gpack.at[k, which, pl.ds(at, size)]
            if dr == 0:
                target = gside.at[k, 1 - which]
            else:
                target = gcorner.at[k, 1 - which, 0 if dr > 0 else 1]
        return pltpu.make_async_remote_copy(
            src_ref=source, dst_ref=target, send_sem=grad_send.at[k, n], recv_sem=grad_recv.at[k, n],
            device_id=(row + dr, col + dc), device_id_type=MESH)

    def start_all(make):
        for dr, dc in around:
            @pl.when(inside(dr, dc))
            def _(dr=dr, dc=dc):
                make(dr, dc).start()

    def wait_all(make, send):
        for dr, dc in around:
            if send:
                @pl.when(inside(dr, dc))
                def _(dr=dr, dc=dc):
                    make(dr, dc).wait_send()
            else:
                @pl.when(inside(-dr, -dc))
                def _(dr=dr, dc=dc):
                    make(dr, dc).wait_recv()

    pack_tile(0, obj_ref)
    tall = 1 + (row > 0).astype(jnp.int32) + (row < rows - 1).astype(jnp.int32)
    broad = 1 + (col > 0).astype(jnp.int32) + (col < cols - 1).astype(jnp.int32)
    pl.semaphore_wait(barrier, tall * broad - 1 + planes + lines - 1)
    start_all(lambda dr, dc: halo_copy(0, obj_ref, dr, dc))

    for n, (a, b) in enumerate(((a_hi, b_hi), (a_lo, b_lo))):
        real, imag = tables_ref[n], tables_ref[2 + n]
        lo, hi = pl.ds(0, frame), pl.ds(frame, frame)
        for ref, sign in ((a, 1), (b, -1)):
            ref[lo, lo] = real
            ref[hi, hi] = real
            ref[lo, hi] = -imag if sign > 0 else imag
            ref[hi, lo] = imag if sign > 0 else -imag
    half = frame // LANES
    for c in range(2):
        ext[0, c, H:H + tile, LANES:LANES + tile] = obj_ref[c]
        for m in range(modes):
            for h in range(half):
                weights[0, pl.ds(((c * modes + m) * half + h) * frame, frame)] = (
                    probe_ref[c, m, :, h * LANES:(h + 1) * LANES])

    def probe_part(k, c, m):
        base = (c * modes + m) * half
        return jnp.concatenate(
            [weights[k, pl.ds((base + h) * frame, frame)] for h in range(half)], axis=1)

    oy, ox = off_ref[0, 0, 0, 0], off_ref[0, 0, 0, 1] + (LANES - H)
    for ref, outer, shift in (
        (row_pick, 0, oy), (row_place, 1, oy), (col_pick, 1, ox), (col_place, 0, ox)
    ):
        inner_at = lax.broadcasted_iota(jnp.int32, ref.shape, outer)
        outer_at = lax.broadcasted_iota(jnp.int32, ref.shape, 1 - outer)
        ref[...] = jnp.where(outer_at == inner_at + shift, 1.0, 0.0).astype(bf16)

    for k in range(ITERS):
        source = obj_ref if k == 0 else current
        wait_all(lambda dr, dc: halo_copy(k, source, dr, dc), False)
        for s, at in ((0, 0), (1, LANES + tile)):
            block = side[k, s]
            other = pltpu.roll(block, H, 1)
            first, second = (block, other)
            ext[k, 0, :, at:at + LANES] = first
            ext[k, 1, :, at:at + LANES] = second
        patch = [
            pick(split(pick(row_pick, split(ext[k, c]))), col_pick)
            for c in range(2)
        ]

        def cut(m):
            return pl.ds(m * frame, frame)

        for m in range(modes):
            p_re, p_im = probe_part(k, 0, m), probe_part(k, 1, m)
            for c, wave in enumerate((p_re * patch[0] - p_im * patch[1], p_re * patch[1] + p_im * patch[0])):
                x_hi[cut(c), cut(m)], x_lo[cut(c), cut(m)] = split(wave)
        out = product((a_hi, a_lo), (x_hi, x_lo))
        for m in range(modes):
            for c in range(2):
                part = out[c * frame:(c + 1) * frame, m * frame:(m + 1) * frame]
                x_hi[cut(m), cut(c)], x_lo[cut(m), cut(c)] = split(part)
        far = product((x_hi, x_lo), (b_hi, b_lo))
        far = [[far[m * frame:(m + 1) * frame, c * frame:(c + 1) * frame] for c in range(2)] for m in range(modes)]
        intensity = sum(re * re + im * im for re, im in far)
        factor = 1.0 - amp_ref[0, 0, 0] / jnp.sqrt(intensity + 1.0)
        for m in range(modes):
            for c in range(2):
                x_hi[cut(m), cut(c)], x_lo[cut(m), cut(c)] = split(far[m][c] * factor)
        out = product((x_hi, x_lo), (a_hi, a_lo))
        for m in range(modes):
            for c in range(2):
                part = out[m * frame:(m + 1) * frame, c * frame:(c + 1) * frame]
                x_hi[cut(c), cut(m)], x_lo[cut(c), cut(m)] = split(part)
        back = product((b_hi, b_lo), (x_hi, x_lo))
        back = [[back[c * frame:(c + 1) * frame, m * frame:(m + 1) * frame] for c in range(2)] for m in range(modes)]

        for m in range(modes):
            re, im = back[m]
            for c, term in enumerate((patch[0] * re + patch[1] * im, patch[0] * im - patch[1] * re)):
                for h in range(half):
                    terms[k, pl.ds(((c * modes + m) * half + h) * frame, frame)] = term[:, h * LANES:(h + 1) * LANES]
        n1 = terms.shape[1] // 2
        n3 = n1 // (planes * lines)
        size = planes * n3
        mine, theirs = core * n1, (1 - core) * n1
        slots = iter(range(sum_send.shape[1]))
        pending = []

        def rows_at(at, n):
            return pl.ds(pl.multiple_of(at, 8), n)

        def remote(src, dst, device):
            slot = next(slots)
            copy = pltpu.make_async_remote_copy(
                src_ref=src, dst_ref=dst, send_sem=sum_send.at[k, slot], recv_sem=sum_recv.at[k, slot],
                device_id=device, device_id_type=MESH)
            copy.start()
            pending.append(copy)
            return copy

        far_first = list(range(lines - 1, -1, -1))
        blocks = [line_peer(d)[1] * size for d in range(lines)]
        swaps = {
            d: remote(terms.at[k, rows_at(theirs + blocks[d], size)], r1.at[k, rows_at(blocks[d], size)], partner)
            for d in far_first
        }

        for c in range(2):
            acc = None
            for m in range(modes):
                p_re, p_im = probe_part(k, 0, m), probe_part(k, 1, m)
                re, im = back[m]
                term = p_re * re + p_im * im if c == 0 else p_re * im - p_im * re
                acc = term if acc is None else acc + term
            grad[k, c] = pick(split(pick(row_place, split(acc))), col_place)
        gpack[k, 0] = paired(upper, grad[k, 0, :, :LANES], grad[k, 1, :, :LANES])
        gpack[k, 1] = paired(lower, grad[k, 0, :, LANES + tile:], grad[k, 1, :, LANES + tile:])

        scatter2 = {}
        for d in far_first:
            swaps[d].wait_recv()
            a1[k, rows_at(blocks[d], size)] = terms[k, rows_at(mine + blocks[d], size)] + r1[k, rows_at(blocks[d], size)]
            scatter2[d] = []
            for e in range(1, planes):
                device, other = plane_peer(e)
                scatter2[d].append(remote(a1.at[k, rows_at(blocks[d] + other * n3, n3)], r2.at[k, e - 1, d], device))
        start_all(lambda dr, dc: grad_copy(k, dr, dc))

        scatter3 = []
        for d in far_first:
            value = a1[k, rows_at(blocks[d] + plane * n3, n3)]
            for e in range(1, planes):
                scatter2[d][e - 1].wait_recv()
                value = value + r2[k, e - 1, d]
            if d:
                a2[k, d - 1] = value
                scatter3.append((d, remote(a2.at[k, d - 1], r3.at[k, d - 1], line_peer(d)[0])))
        for d, copy in scatter3:
            copy.wait_recv()
            value = value + r3[k, d - 1]
        own = rows_at(mine + blocks[0] + plane * n3, n3)
        weights[k + 1, own] = weights[k, own] - coeff * value

        def chunk(d):
            return weights.at[k + 1, rows_at(mine + blocks[d] + plane * n3, n3)]

        gather3 = {d: remote(chunk(0), chunk(0), line_peer(d)[0]) for d in far_first[:-1]}
        gather2 = {0: [remote(chunk(0), chunk(0), plane_peer(e)[0]) for e in range(1, planes)]}

        wait_all(lambda dr, dc: grad_copy(k, dr, dc), False)
        target = current if k + 1 < ITERS else new_obj_ref
        for s in range(2):
            mask, at = ((lower, 0), (upper, tile - LANES))[s]
            block = gside[k, s]
            block = jnp.concatenate(
                [block[:H] + gcorner[k, s, 0], block[H:tile - H], block[tile - H:] + gcorner[k, s, 1]], axis=0)
            where = pl.ds(LANES + at, LANES)
            grad[k, 0, H:H + tile, where] += jnp.where(mask, block, 0.0)
            grad[k, 1, H:H + tile, where] += jnp.where(mask, pltpu.roll(block, H, 1), 0.0)
        grad[k, :, H:2 * H, LANES:LANES + tile] += grows[k, 0]
        grad[k, :, tile:tile + H, LANES:LANES + tile] += grows[k, 1]
        for c in range(2):
            target[c] = source[c] - object_step * grad[k, c, H:H + tile, LANES:LANES + tile]
        if k + 1 < ITERS:
            pack_tile(k + 1, current)
            start_all(lambda dr, dc: halo_copy(k + 1, current, dr, dc))
            for c in range(2):
                ext[k + 1, c, H:H + tile, LANES:LANES + tile] = current[c]

        for d in range(1, lines):
            gather3[d].wait_recv()
            gather2[d] = [remote(chunk(d), chunk(d), plane_peer(e)[0]) for e in range(1, planes)]
        back1 = []
        for d in range(lines):
            for copy in gather2[d]:
                copy.wait_recv()
            block = weights.at[k + 1, rows_at(mine + blocks[d], size)]
            back1.append(remote(block, block, partner))
        for copy in back1:
            copy.wait_recv()
        for copy in pending:
            copy.wait_send()
        wait_all(lambda dr, dc: halo_copy(k, source, dr, dc), True)
        wait_all(lambda dr, dc: grad_copy(k, dr, dc), True)

    for c in range(2):
        for m in range(modes):
            new_probe_ref[c, m] = probe_part(ITERS, c, m)


def local(rows, cols, object_field, probe, amplitudes, offsets):
    frame = amplitudes.shape[-1]
    tile = object_field.shape[1]
    modes = probe.shape[1]
    span, width = tile + 2 * H, tile + 2 * LANES
    tables = jnp.asarray(dft_tables(frame))
    total = 2 * modes * frame * (frame // LANES)
    planes, lines = rows * 2, cols // 4
    n1 = total // 2
    n3 = n1 // (planes * lines)
    copies = 2 * (lines * planes + lines - 1)
    f32 = jnp.float32
    wide = 2 * frame
    vmem = pl.BlockSpec(memory_space=pltpu.VMEM)
    dma = pltpu.SemaphoreType.DMA
    return pl.pallas_call(
        functools.partial(kernel, rows, cols),
        out_shape=(
            jax.ShapeDtypeStruct(object_field.shape, f32),
            jax.ShapeDtypeStruct(probe.shape, f32),
        ),
        in_specs=[vmem] * 4 + [pl.BlockSpec(memory_space=pltpu.SMEM)],
        out_specs=(vmem, vmem),
        scratch_shapes=[
            *[pltpu.VMEM((wide, wide), bf16)] * 4,
            *[pltpu.VMEM((wide, modes * frame), bf16)] * 2,
            pltpu.VMEM((frame, span), bf16),
            pltpu.VMEM((width, frame), bf16),
            pltpu.VMEM((span, frame), bf16),
            pltpu.VMEM((frame, width), bf16),
            pltpu.VMEM((ITERS, 2, span, width), f32),
            pltpu.VMEM((ITERS, 2, span, LANES), f32),
            pltpu.VMEM((ITERS, 2, tile, LANES), f32),
            pltpu.VMEM((ITERS, 2, span, width), f32),
            pltpu.VMEM((ITERS, 2, span, LANES), f32),
            pltpu.VMEM((ITERS, 2, 2, H, tile), f32),
            pltpu.VMEM((ITERS, 2, tile, LANES), f32),
            pltpu.VMEM((ITERS, 2, 2, H, LANES), f32),
            pltpu.VMEM((2, tile, tile), f32),
            pltpu.VMEM((ITERS, total, LANES), f32),
            pltpu.VMEM((ITERS, n1, LANES), f32),
            pltpu.VMEM((ITERS, n1, LANES), f32),
            pltpu.VMEM((ITERS, planes - 1, lines, n3, LANES), f32),
            pltpu.VMEM((ITERS, lines - 1, n3, LANES), f32),
            pltpu.VMEM((ITERS, lines - 1, n3, LANES), f32),
            pltpu.VMEM((ITERS + 1, total, LANES), f32),
            dma((ITERS, 8)), dma((ITERS, 8)), dma((ITERS, 8)), dma((ITERS, 8)),
            dma((ITERS, copies)), dma((ITERS, copies)),
        ],
        compiler_params=pltpu.CompilerParams(
            collective_id=0, has_side_effects=True, vmem_limit_bytes=60 * 1024 * 1024
        ),
    )(object_field, probe, amplitudes, tables, offsets)


def solution(mesh):
    rows, cols = mesh.shape["row"], mesh.shape["col"]

    def body(*args):
        return local(rows, cols, *args)

    return jax.shard_map(
        body,
        mesh=mesh,
        in_specs=(
            P(None, "row", "col"),
            P(),
            P("row", "col", None, None, None),
            P("row", "col", None, None),
        ),
        out_specs=(P(None, "row", "col"), P()),
        check_vma=False,
    )
```

```python
import functools
import math

import jax
import jax.numpy as jnp
import numpy as np
from jax import lax
from jax.experimental import pallas as pl
from jax.experimental.pallas import tpu as pltpu
from jax.sharding import PartitionSpec as P

H = 64
LANES = 128
ITERS = 2
object_step = 0.25
probe_step = 4.0
MESH = pl.DeviceIdType.MESH
bf16 = jnp.bfloat16


def dft_tables(length):
    counter = np.arange(length)
    angle = -2.0 * math.pi / length * (counter[:, None] * counter[None, :] % length)
    scale = 1.0 / math.sqrt(length)
    parts = []
    for table in (np.cos(angle) * scale, np.sin(angle) * scale):
        table = table.astype(np.float32)
        high = table.astype(bf16)
        low = (table - high.astype(np.float32)).astype(bf16)
        parts += [high, low]
    return np.stack(parts)


def split(value):
    high = value.astype(bf16)
    return high, (value - high.astype(jnp.float32)).astype(bf16)


def product(left, right):
    out = jnp.dot(left[0][...], right[0][...], preferred_element_type=jnp.float32)
    out += jnp.dot(left[0][...], right[1][...], preferred_element_type=jnp.float32)
    return out + jnp.dot(left[1][...], right[0][...], preferred_element_type=jnp.float32)


def pick(one_hot, value):
    if isinstance(value, tuple):
        return sum(jnp.dot(one_hot[...], v, preferred_element_type=jnp.float32) for v in value)
    return sum(jnp.dot(v, value[...], preferred_element_type=jnp.float32) for v in one_hot)


def kernel(
    rows, cols, obj_in, probe_in, amp_in, tables_in, off_ref,
    new_obj_ref, new_probe_ref,
    a_hi, a_lo, b_hi, b_lo, x_hi, x_lo,
    row_pick, col_pick, row_place, col_place, ext, side, pack, grad, gpack, grows, gside, gcorner, current,
    terms, r1, a1, r2, a2, r3, weights,
    amp_ref, tables_ref, in_sem, out_sem,
    halo_send, halo_recv, grad_send, grad_recv, sum_send, sum_recv,
):
    frame = amp_in.shape[-1]
    tile = obj_in.shape[1]
    modes = probe_in.shape[1]
    half = frame // LANES
    span = tile + 2 * H
    row, col = lax.axis_index("row"), lax.axis_index("col")
    coeff = probe_step / (rows * cols)
    core = lax.rem(col, 2)
    plane = row * 2 + lax.rem(col // 2, 2)
    line = col // 4
    planes, lines = rows * 2, cols // 4

    around = [(dr, dc) for dr in (-1, 0, 1) for dc in (-1, 0, 1) if (dr, dc) != (0, 0)]

    def inside(dr, dc):
        r, c = row + dr, col + dc
        ok = jnp.bool_(True)
        if dr:
            ok = (r >= 0) & (r < rows)
        if dc:
            ok = ok & (c >= 0) & (c < cols)
        return ok

    def flip(index, d):
        bit = 1
        while bit <= d:
            if d & bit:
                index = index + bit * (1 - 2 * lax.rem(index // bit, 2))
            bit *= 2
        return index

    def plane_peer(d):
        other = flip(plane, d)
        return (other // 2, line * 4 + lax.rem(other, 2) * 2 + core), other

    def line_peer(d):
        other = flip(line, d)
        return (row, other * 4 + lax.rem(col, 4)), other

    partner = (row, col + 1 - 2 * core)

    def strip(ref, c, m, h):
        return ref.at[c, m, :, pl.ds(h * LANES, LANES)]

    def strip_rows(c, m, h):
        return pl.ds(((c * modes + m) * half + h) * frame, frame)

    strips = [(m, h) for m in range(modes) for h in range(half)]
    load_obj = pltpu.make_async_copy(obj_in, current.at[0], in_sem.at[0])
    loads = [
        pltpu.make_async_copy(tables_in, tables_ref, in_sem.at[1]),
        pltpu.make_async_copy(amp_in.at[0, 0, 0], amp_ref, in_sem.at[2]),
    ]
    for c in range(2):
        for n, (m, h) in enumerate(strips):
            loads.append(pltpu.make_async_copy(
                strip(probe_in, c, m, h), weights.at[0, strip_rows(c, m, h)],
                in_sem.at[3 + c * len(strips) + n]))
    load_obj.start()
    for copy in loads:
        copy.start()

    barrier = pltpu.get_barrier_semaphore()
    for dr, dc in around:
        @pl.when(inside(dr, dc))
        def _(dr=dr, dc=dc):
            pl.semaphore_signal(barrier, inc=1, device_id=(row + dr, col + dc), device_id_type=MESH)
    pl.semaphore_signal(barrier, inc=1, device_id=partner, device_id_type=MESH)
    for d in range(1, planes):
        pl.semaphore_signal(barrier, inc=1, device_id=plane_peer(d)[0], device_id_type=MESH)
    for d in range(1, lines):
        pl.semaphore_signal(barrier, inc=1, device_id=line_peer(d)[0], device_id_type=MESH)

    lane = lax.broadcasted_iota(jnp.int32, (1, LANES), 1)
    lower, upper = lane < H, lane >= H

    def paired(mask, real, imag):
        return jnp.where(mask, real, pltpu.roll(imag, H, 1))

    def pack_tile(k, src):
        pack[k, 0] = paired(lower, src[0, :, :LANES], src[1, :, :LANES])
        pack[k, 1] = paired(upper, src[0, :, tile - LANES:], src[1, :, tile - LANES:])

    def halo_ends(k, src, dr, dc):
        if dc == 0:
            source = src.at[:, pl.ds(0 if dr < 0 else tile - H, H), :]
            target = ext.at[k, :, pl.ds(tile + H if dr < 0 else 0, H), pl.ds(LANES, tile)]
        else:
            which = 0 if dc < 0 else 1
            at, size = {-1: (0, H), 0: (0, tile), 1: (tile - H, H)}[dr]
            source = pack.at[k, which, pl.ds(at, size)]
            target = side.at[k, 1 - which, pl.ds({-1: tile + H, 0: H, 1: 0}[dr], size)]
        return source, target

    def halo_copy(k, src, dr, dc):
        n = around.index((dr, dc))
        source, target = halo_ends(k, src, dr, dc)
        return pltpu.make_async_remote_copy(
            src_ref=source, dst_ref=target, send_sem=halo_send.at[k, n], recv_sem=halo_recv.at[k, n],
            device_id=(row + dr, col + dc), device_id_type=MESH)

    def grad_ends(k, dr, dc):
        if dc == 0:
            source = grad.at[k, :, pl.ds(0 if dr < 0 else tile + H, H), pl.ds(LANES, tile)]
            target = grows.at[k, 0 if dr > 0 else 1]
        else:
            which = 0 if dc < 0 else 1
            at, size = {-1: (0, H), 0: (H, tile), 1: (tile + H, H)}[dr]
            source = gpack.at[k, which, pl.ds(at, size)]
            if dr == 0:
                target = gside.at[k, 1 - which]
            else:
                target = gcorner.at[k, 1 - which, 0 if dr > 0 else 1]
        return source, target

    def grad_copy(k, dr, dc):
        n = around.index((dr, dc))
        source, target = grad_ends(k, dr, dc)
        return pltpu.make_async_remote_copy(
            src_ref=source, dst_ref=target, send_sem=grad_send.at[k, n], recv_sem=grad_recv.at[k, n],
            device_id=(row + dr, col + dc), device_id_type=MESH)

    def start_all(make):
        for dr, dc in around:
            @pl.when(inside(dr, dc))
            def _(dr=dr, dc=dc):
                make(dr, dc).start()

    def wait_all(make, send):
        for dr, dc in around:
            if send:
                @pl.when(inside(dr, dc))
                def _(dr=dr, dc=dc):
                    make(dr, dc).wait_send()
            else:
                @pl.when(inside(-dr, -dc))
                def _(dr=dr, dc=dc):
                    make(dr, dc).wait_recv()

    load_obj.wait()
    pack_tile(0, current.at[0])
    tall = 1 + (row > 0).astype(jnp.int32) + (row < rows - 1).astype(jnp.int32)
    broad = 1 + (col > 0).astype(jnp.int32) + (col < cols - 1).astype(jnp.int32)
    pl.semaphore_wait(barrier, tall * broad - 1 + planes + lines - 1)
    start_all(lambda dr, dc: halo_copy(0, current.at[0], dr, dc))

    def zero(ref):
        ref[...] = jnp.zeros_like(ref)

    for dr, dc in around:
        @pl.when(jnp.logical_not(inside(-dr, -dc)))
        def _(dr=dr, dc=dc):
            for k in range(ITERS):
                zero(halo_ends(k, current.at[0], dr, dc)[1])
                zero(grad_ends(k, dr, dc)[1])

    for copy in loads:
        copy.wait()
    for n, (a, b) in enumerate(((a_hi, b_hi), (a_lo, b_lo))):
        real, imag = tables_ref[n], tables_ref[2 + n]
        lo, hi = pl.ds(0, frame), pl.ds(frame, frame)
        for ref, sign in ((a, 1), (b, -1)):
            ref[lo, lo] = real
            ref[hi, hi] = real
            ref[lo, hi] = -imag if sign > 0 else imag
            ref[hi, lo] = imag if sign > 0 else -imag
    for c in range(2):
        ext[0, c, H:H + tile, LANES:LANES + tile] = current[0, c]

    def probe_part(k, c, m):
        base = (c * modes + m) * half
        return jnp.concatenate(
            [weights[k, pl.ds((base + h) * frame, frame)] for h in range(half)], axis=1)

    oy, ox = off_ref[0, 0, 0, 0], off_ref[0, 0, 0, 1] + (LANES - H)
    for ref, outer, shift in (
        (row_pick, 0, oy), (row_place, 1, oy), (col_pick, 1, ox), (col_place, 0, ox)
    ):
        inner_at = lax.broadcasted_iota(jnp.int32, ref.shape, outer)
        outer_at = lax.broadcasted_iota(jnp.int32, ref.shape, 1 - outer)
        ref[...] = jnp.where(outer_at == inner_at + shift, 1.0, 0.0).astype(bf16)

    for k in range(ITERS):
        source = current.at[k]
        wait_all(lambda dr, dc: halo_copy(k, source, dr, dc), False)
        for s, at in ((0, 0), (1, LANES + tile)):
            block = side[k, s]
            other = pltpu.roll(block, H, 1)
            first, second = (block, other)
            ext[k, 0, :, at:at + LANES] = first
            ext[k, 1, :, at:at + LANES] = second
        patch = [
            pick(split(pick(row_pick, split(ext[k, c]))), col_pick)
            for c in range(2)
        ]

        def cut(m):
            return pl.ds(m * frame, frame)

        for m in range(modes):
            p_re, p_im = probe_part(k, 0, m), probe_part(k, 1, m)
            for c, wave in enumerate((p_re * patch[0] - p_im * patch[1], p_re * patch[1] + p_im * patch[0])):
                x_hi[cut(c), cut(m)], x_lo[cut(c), cut(m)] = split(wave)
        out = product((a_hi, a_lo), (x_hi, x_lo))
        for m in range(modes):
            for c in range(2):
                part = out[c * frame:(c + 1) * frame, m * frame:(m + 1) * frame]
                x_hi[cut(m), cut(c)], x_lo[cut(m), cut(c)] = split(part)
        far = product((x_hi, x_lo), (b_hi, b_lo))
        far = [[far[m * frame:(m + 1) * frame, c * frame:(c + 1) * frame] for c in range(2)] for m in range(modes)]
        intensity = sum(re * re + im * im for re, im in far)
        factor = 1.0 - amp_ref[...] / jnp.sqrt(intensity + 1.0)
        for m in range(modes):
            for c in range(2):
                x_hi[cut(m), cut(c)], x_lo[cut(m), cut(c)] = split(far[m][c] * factor)
        out = product((x_hi, x_lo), (a_hi, a_lo))
        for m in range(modes):
            for c in range(2):
                part = out[m * frame:(m + 1) * frame, c * frame:(c + 1) * frame]
                x_hi[cut(c), cut(m)], x_lo[cut(c), cut(m)] = split(part)
        back = product((b_hi, b_lo), (x_hi, x_lo))
        back = [[back[c * frame:(c + 1) * frame, m * frame:(m + 1) * frame] for c in range(2)] for m in range(modes)]

        for m in range(modes):
            re, im = back[m]
            for c, term in enumerate((patch[0] * re + patch[1] * im, patch[0] * im - patch[1] * re)):
                for h in range(half):
                    terms[k, pl.ds(((c * modes + m) * half + h) * frame, frame)] = term[:, h * LANES:(h + 1) * LANES]
        n1 = terms.shape[1] // 2
        n3 = n1 // (planes * lines)
        size = planes * n3
        mine, theirs = core * n1, (1 - core) * n1
        slots = iter(range(sum_send.shape[1]))
        pending = []

        def rows_at(at, n):
            return pl.ds(pl.multiple_of(at, 8), n)

        def remote(src, dst, device):
            slot = next(slots)
            copy = pltpu.make_async_remote_copy(
                src_ref=src, dst_ref=dst, send_sem=sum_send.at[k, slot], recv_sem=sum_recv.at[k, slot],
                device_id=device, device_id_type=MESH)
            copy.start()
            pending.append(copy)
            return copy

        far_first = list(range(lines - 1, -1, -1))
        blocks = [line_peer(d)[1] * size for d in range(lines)]
        swaps = {
            d: remote(terms.at[k, rows_at(theirs + blocks[d], size)], r1.at[k, rows_at(blocks[d], size)], partner)
            for d in far_first
        }

        for c in range(2):
            acc = None
            for m in range(modes):
                p_re, p_im = probe_part(k, 0, m), probe_part(k, 1, m)
                re, im = back[m]
                term = p_re * re + p_im * im if c == 0 else p_re * im - p_im * re
                acc = term if acc is None else acc + term
            grad[k, c] = pick(split(pick(row_place, split(acc))), col_place)
        gpack[k, 0] = paired(upper, grad[k, 0, :, :LANES], grad[k, 1, :, :LANES])
        gpack[k, 1] = paired(lower, grad[k, 0, :, LANES + tile:], grad[k, 1, :, LANES + tile:])

        scatter2 = {}
        for d in far_first:
            swaps[d].wait_recv()
            a1[k, rows_at(blocks[d], size)] = terms[k, rows_at(mine + blocks[d], size)] + r1[k, rows_at(blocks[d], size)]
            scatter2[d] = []
            for e in range(1, planes):
                device, other = plane_peer(e)
                scatter2[d].append(remote(a1.at[k, rows_at(blocks[d] + other * n3, n3)], r2.at[k, e - 1, d], device))
        start_all(lambda dr, dc: grad_copy(k, dr, dc))

        scatter3 = []
        for d in far_first:
            value = a1[k, rows_at(blocks[d] + plane * n3, n3)]
            for e in range(1, planes):
                scatter2[d][e - 1].wait_recv()
                value = value + r2[k, e - 1, d]
            if d:
                a2[k, d - 1] = value
                scatter3.append((d, remote(a2.at[k, d - 1], r3.at[k, d - 1], line_peer(d)[0])))
        for d, copy in scatter3:
            copy.wait_recv()
            value = value + r3[k, d - 1]
        own = rows_at(mine + blocks[0] + plane * n3, n3)
        weights[k + 1, own] = weights[k, own] - coeff * value

        def chunk(d):
            return weights.at[k + 1, rows_at(mine + blocks[d] + plane * n3, n3)]

        gather3 = {d: remote(chunk(0), chunk(0), line_peer(d)[0]) for d in far_first[:-1]}
        gather2 = {0: [remote(chunk(0), chunk(0), plane_peer(e)[0]) for e in range(1, planes)]}

        wait_all(lambda dr, dc: grad_copy(k, dr, dc), False)
        target = current.at[k + 1]
        for s in range(2):
            mask, at = ((lower, 0), (upper, tile - LANES))[s]
            block = gside[k, s]
            block = jnp.concatenate(
                [block[:H] + gcorner[k, s, 0], block[H:tile - H], block[tile - H:] + gcorner[k, s, 1]], axis=0)
            where = pl.ds(LANES + at, LANES)
            grad[k, 0, H:H + tile, where] += jnp.where(mask, block, 0.0)
            grad[k, 1, H:H + tile, where] += jnp.where(mask, pltpu.roll(block, H, 1), 0.0)
        grad[k, :, H:2 * H, LANES:LANES + tile] += grows[k, 0]
        grad[k, :, tile:tile + H, LANES:LANES + tile] += grows[k, 1]
        for c in range(2):
            target[c] = source[c] - object_step * grad[k, c, H:H + tile, LANES:LANES + tile]
        if k + 1 < ITERS:
            pack_tile(k + 1, target)
            start_all(lambda dr, dc: halo_copy(k + 1, target, dr, dc))
            for c in range(2):
                ext[k + 1, c, H:H + tile, LANES:LANES + tile] = target[c]
        else:
            store_obj = pltpu.make_async_copy(target, new_obj_ref, out_sem.at[0])
            store_obj.start()
        for d in range(1, lines):
            gather3[d].wait_recv()
            gather2[d] = [remote(chunk(d), chunk(d), plane_peer(e)[0]) for e in range(1, planes)]
        back1 = []
        for d in range(lines):
            for copy in gather2[d]:
                copy.wait_recv()
            block = weights.at[k + 1, rows_at(mine + blocks[d], size)]
            back1.append(remote(block, block, partner))
        if k + 1 == ITERS:
            stores = [
                pltpu.make_async_copy(
                    weights.at[ITERS, strip_rows(core, m, h)], strip(new_probe_ref, core, m, h), out_sem.at[1 + n])
                for n, (m, h) in enumerate(strips)
            ]
            for copy in stores:
                copy.start()
        for copy in back1:
            copy.wait_recv()
        for copy in pending:
            copy.wait_send()
        wait_all(lambda dr, dc: halo_copy(k, source, dr, dc), True)
        wait_all(lambda dr, dc: grad_copy(k, dr, dc), True)

    for n, (m, h) in enumerate(strips):
        copy = pltpu.make_async_copy(
            weights.at[ITERS, strip_rows(1 - core, m, h)], strip(new_probe_ref, 1 - core, m, h),
            out_sem.at[1 + len(strips) + n])
        copy.start()
        stores.append(copy)
    store_obj.wait()
    for copy in stores:
        copy.wait()


def local(rows, cols, object_field, probe, amplitudes, offsets):
    frame = amplitudes.shape[-1]
    tile = object_field.shape[1]
    modes = probe.shape[1]
    span, width = tile + 2 * H, tile + 2 * LANES
    tables = jnp.asarray(dft_tables(frame))
    total = 2 * modes * frame * (frame // LANES)
    planes, lines = rows * 2, cols // 4
    n1 = total // 2
    n3 = n1 // (planes * lines)
    copies = 2 * (lines * planes + lines - 1)
    f32 = jnp.float32
    wide = 2 * frame
    anywhere = pl.BlockSpec(memory_space=pl.ANY)
    strips = modes * (frame // LANES)
    dma = pltpu.SemaphoreType.DMA
    return pl.pallas_call(
        functools.partial(kernel, rows, cols),
        out_shape=(
            jax.ShapeDtypeStruct(object_field.shape, f32),
            jax.ShapeDtypeStruct(probe.shape, f32),
        ),
        in_specs=[anywhere] * 4 + [pl.BlockSpec(memory_space=pltpu.SMEM)],
        out_specs=(anywhere, anywhere),
        scratch_shapes=[
            *[pltpu.VMEM((wide, wide), bf16)] * 4,
            *[pltpu.VMEM((wide, modes * frame), bf16)] * 2,
            pltpu.VMEM((frame, span), bf16),
            pltpu.VMEM((width, frame), bf16),
            pltpu.VMEM((span, frame), bf16),
            pltpu.VMEM((frame, width), bf16),
            pltpu.VMEM((ITERS, 2, span, width), f32),
            pltpu.VMEM((ITERS, 2, span, LANES), f32),
            pltpu.VMEM((ITERS, 2, tile, LANES), f32),
            pltpu.VMEM((ITERS, 2, span, width), f32),
            pltpu.VMEM((ITERS, 2, span, LANES), f32),
            pltpu.VMEM((ITERS, 2, 2, H, tile), f32),
            pltpu.VMEM((ITERS, 2, tile, LANES), f32),
            pltpu.VMEM((ITERS, 2, 2, H, LANES), f32),
            pltpu.VMEM((ITERS + 1, 2, tile, tile), f32),
            pltpu.VMEM((ITERS, total, LANES), f32),
            pltpu.VMEM((ITERS, n1, LANES), f32),
            pltpu.VMEM((ITERS, n1, LANES), f32),
            pltpu.VMEM((ITERS, planes - 1, lines, n3, LANES), f32),
            pltpu.VMEM((ITERS, lines - 1, n3, LANES), f32),
            pltpu.VMEM((ITERS, lines - 1, n3, LANES), f32),
            pltpu.VMEM((ITERS + 1, total, LANES), f32),
            pltpu.VMEM((frame, frame), f32),
            pltpu.VMEM((4, frame, frame), bf16),
            dma((3 + 2 * strips,)), dma((1 + 2 * strips,)),
            dma((ITERS, 8)), dma((ITERS, 8)), dma((ITERS, 8)), dma((ITERS, 8)),
            dma((ITERS, copies)), dma((ITERS, copies)),
        ],
        compiler_params=pltpu.CompilerParams(
            collective_id=0, has_side_effects=True, vmem_limit_bytes=60 * 1024 * 1024
        ),
    )(object_field, probe, amplitudes, tables, offsets)


def solution(mesh):
    rows, cols = mesh.shape["row"], mesh.shape["col"]

    def body(*args):
        return local(rows, cols, *args)

    return jax.shard_map(
        body,
        mesh=mesh,
        in_specs=(
            P(None, "row", "col"),
            P(),
            P("row", "col", None, None, None),
            P("row", "col", None, None),
        ),
        out_specs=(P(None, "row", "col"), P()),
        check_vma=False,
    )
```
